32 devices in a mesh: lat: 4 (over x, core), lon: 8 (over z, y).
Axes of the slice: x: 2, y: 2, z: 4, core: 2. Of those that a mesh axis runs over, the one named last changes fastest.
Arguments:
- node_latent: bfloat16 [64, 256, 512], P('lat', 'lon'), may hold values from -6 to 6
- edge_latent: bfloat16 [65536, 512], P(('lat', 'lon')), may hold values from -6 to 6
- sender: int32 [65536], P(('lat', 'lon')), may hold values from -1 to 16383, as said below
- receiver: int32 [65536], P(('lat', 'lon')), may hold values from -1 to 127, as said below
- block_tile: int32 [512], P(('lat', 'lon')), may hold values from 0 to 3, as said below
- w_first: bfloat16 [1536, 512], replicated, may hold values from -0.15625 to 0.15625
- w_second: bfloat16 [512, 512], replicated, may hold values from -0.25 to 0.25
- edge_gain: float32 [512], replicated, may hold values from 0.5 to 1.5
- w_node_first: bfloat16 [1024, 512], replicated, may hold values from -0.1875 to 0.1875
- w_node_second: bfloat16 [512, 512], replicated, may hold values from -0.25 to 0.25
- node_gain: float32 [512], replicated, may hold values from 0.5 to 1.5
Outputs:
- node_out: bfloat16 [64, 256, 512], P('lat', 'lon')
- edge_out: bfloat16 [65536, 512], P(('lat', 'lon'))
The draws below stay inside these ranges and needn't reach their ends.
Inputs may be any that keep to these rules, and one draw needn't show every extreme that they name: `sender`: -1 on padded slots; otherwise the id of one of the eight grid neighbours of the edge's receiver node (columns wrap around, rows do not), or of a node whose row and column are both multiples of 4, anywhere on the grid. `receiver`: padded slots (-1) stand at the end of each block, at least 32 slots of a block are live, and live values never fall within a block. `block_tile`: never falls from one block of a device to the next, over the device's 16 blocks.
All inputs are finite; a program needn't handle non-finite values.
Results may differ from the reference program's by a relative error of at most 0.008.
Values may be sent and summed in bfloat16 or wider, within the bound.
A program may use at most 128 MiB of HBM per device.

```python
import jax
import jax.numpy as jnp
import numpy as np
from jax import lax

D = 512
PR = 16
PC = 32
BLOCKS_DEV = 16
BLK = 128
TILE_NODES = 128
NODE_DEV = 512
EDGE_DEV = 2048
NLAT = 64
NLON = 256
NODES = 16384
EDGES = 65536
N_LAT = 4
N_LON = 8
DEVICES = 32


def edge_plan(key):
    folded = jax.random.fold_in(key, 1013)
    subkeys = jax.random.split(folded, 7)
    grid_rows = PR * N_LAT
    grid_cols = PC * N_LON
    tile_count = PR // 4
    shape = (DEVICES, BLOCKS_DEV, BLK)
    device = jnp.arange(DEVICES, dtype=jnp.int32)[:, None]
    block_pos = jnp.arange(BLOCKS_DEV, dtype=jnp.int32)[None, :]
    offset = jax.random.randint(subkeys[0], (DEVICES, 1), -1, 2)
    tile_of = jnp.clip((block_pos + offset) * tile_count // BLOCKS_DEV, 0, tile_count - 1).astype(jnp.int32)
    live_count = jax.random.randint(subkeys[1], (DEVICES, BLOCKS_DEV, 1), BLK // 4, BLK + 1)
    slot_pos = jnp.arange(BLK, dtype=jnp.int32)[None, None, :]
    live_slot = slot_pos < live_count
    within = jnp.sort(jax.random.randint(subkeys[2], shape, 0, 4 * PC), axis=2)
    receiver = jnp.where(live_slot, within, -1)
    local_index = tile_of[:, :, None] * (4 * PC) + within
    lat_band = (device // N_LON)[:, :, None]
    lon_sector = (device % N_LON)[:, :, None]
    recv_row = lat_band * PR + local_index // PC
    recv_col = lon_sector * PC + local_index % PC
    picked = jax.random.randint(subkeys[3], shape, 0, 8)
    row_table = jnp.array(np.array([-1, -1, -1, 0, 0, 1, 1, 1], np.int32))
    col_table = jnp.array(np.array([-1, 0, 1, -1, 1, -1, 0, 1], np.int32))
    step_row = row_table[picked]
    step_col = col_table[picked]
    near_row = recv_row + step_row
    near_row = jnp.where((near_row < 0) | (near_row >= grid_rows), recv_row - step_row, near_row)
    near_col = (recv_col + step_col) % grid_cols
    is_polar = (lat_band == 0) | (lat_band == N_LAT - 1)
    coin_flip = jax.random.randint(subkeys[4], shape, 0, 4)
    is_far = coin_flip < jnp.where(is_polar, 2, 1)
    coarse_row = 4 * jax.random.randint(subkeys[5], shape, 0, grid_rows // 4)
    coarse_col = 4 * jax.random.randint(subkeys[6], shape, 0, grid_cols // 4)
    sender = jnp.where(is_far, coarse_row * grid_cols + coarse_col, near_row * grid_cols + near_col)
    sender = jnp.where(live_slot, sender, -1)
    return (sender.reshape(-1).astype(jnp.int32), receiver.reshape(-1).astype(jnp.int32), tile_of.reshape(-1))


def draw_sender(key, part):
    return edge_plan(key)[0]


def draw_receiver(key, part):
    return edge_plan(key)[1]


def draw_block_tile(key, part):
    return edge_plan(key)[2]


def shard_levels(stream_key, extent, shards, low, high):
    loudness, own = 1.0, jax.random.fold_in(stream_key, 6)
    for dim, blocks in shards:
        steps = jnp.exp(jax.random.uniform(jax.random.fold_in(own, dim), (blocks,), jnp.float32, low / len(shards), high / len(shards)))
        loudness = loudness * jnp.repeat(steps, extent[dim] // blocks).reshape([-1 if axis == dim else 1 for axis in range(len(extent))])
    return loudness


def noise(own_key, dims, scale, reach, shards=(), held_as=jnp.bfloat16):
    values = jax.random.normal(own_key, dims, jnp.float32) * scale
    if len(shards) > 0:
        values = shard_levels(own_key, dims, shards, -0.22, 0.18) * values
    return jnp.clip(values, min=-reach, max=reach).astype(held_as)


def setup_inputs(seed: int = 0) -> dict:
    keys = jax.random.split(jax.random.key(seed), 12)
    return {
        "node_latent": noise(keys[0], (NLAT, NLON, D), 1.0, 6.0, ((0, 4), (1, 8))),
        "edge_latent": noise(keys[1], (EDGES, D), 1.0, 6.0, ((0, 32),)),
        "sender": draw_sender(jax.random.fold_in(keys[11], 71), 0),
        "receiver": draw_receiver(jax.random.fold_in(keys[11], 71), 0),
        "block_tile": draw_block_tile(jax.random.fold_in(keys[11], 71), 0),
        "w_first": noise(keys[5], (3 * D, D), (3 * D) ** -0.5, 0.15625),
        "w_second": noise(keys[6], (D, D), D ** -0.5, 0.25),
        "edge_gain": jnp.clip(1.0 + 0.1 * jax.random.normal(keys[7], (D,), jnp.float32), 0.5, 1.5),
        "w_node_first": noise(keys[8], (2 * D, D), (2 * D) ** -0.5, 0.1875),
        "w_node_second": noise(keys[9], (D, D), D ** -0.5, 0.25),
        "node_gain": jnp.clip(1.0 + 0.1 * jax.random.normal(keys[10], (D,), jnp.float32), 0.5, 1.5),
    }


def layer_norm(values, gain_vec):
    average = lax.optimization_barrier(jnp.mean(values, -1, keepdims=True))
    centred = values - average
    spread = lax.optimization_barrier(jnp.mean(centred * centred, -1, keepdims=True))
    return centred * lax.rsqrt(spread + 1e-05) * gain_vec

def reference(node_latent, edge_latent, sender, receiver, block_tile, w_first, w_second, edge_gain, w_node_first, w_node_second, node_gain):
    node_rows = node_latent.reshape(NODES, D)
    edge_parts = edge_latent.reshape(DEVICES, EDGE_DEV, D)
    send_parts = sender.reshape(DEVICES, EDGE_DEV)
    recv_parts = receiver.reshape(DEVICES, EDGE_DEV)
    tile_parts = jnp.broadcast_to(block_tile.reshape(DEVICES, BLOCKS_DEV, 1), (DEVICES, BLOCKS_DEV, BLK)).reshape(DEVICES, EDGE_DEV)

    def one_device(pieces):
        edge_rows, senders, receivers, tile_of, device = pieces
        live_slot = receivers >= 0
        local_index = tile_of * TILE_NODES + jnp.maximum(receivers, 0)
        lat_band = device // N_LON
        lon_sector = device % N_LON
        recv_row = lat_band * PR + local_index // PC
        recv_col = lon_sector * PC + local_index % PC
        recv_rows = node_rows[recv_row * NLON + recv_col]
        send_rows = node_rows[jnp.maximum(senders, 0)]
        joined = jnp.concatenate([edge_rows, send_rows, recv_rows], axis=1)
        first_sum = jnp.dot(joined, w_first, preferred_element_type=jnp.float32)
        hidden = jax.nn.silu(first_sum).astype(jnp.bfloat16)
        second_sum = jnp.dot(hidden, w_second, preferred_element_type=jnp.float32)
        message = layer_norm(second_sum, edge_gain).astype(jnp.bfloat16)
        updated = jnp.where(live_slot[:, None], edge_rows.astype(jnp.float32) + message.astype(jnp.float32), jnp.zeros((), jnp.float32)).astype(jnp.bfloat16)
        segment = jnp.where(live_slot, local_index, NODE_DEV).astype(jnp.int32)
        summed = jax.ops.segment_sum(message.astype(jnp.float32), segment, num_segments=NODE_DEV + 1)[:NODE_DEV]
        return (updated, summed)
    device_ids = jnp.arange(DEVICES, dtype=jnp.int32)
    updated, summed = lax.map(one_device, (edge_parts, send_parts, recv_parts, tile_parts, device_ids))
    aggregate = summed.reshape(N_LAT, N_LON, PR, PC, D).transpose(0, 2, 1, 3, 4).reshape(NODES, D).astype(jnp.bfloat16)
    node_join = jnp.concatenate([node_rows, aggregate], axis=1)
    node_hidden = jax.nn.silu(jnp.dot(node_join, w_node_first, preferred_element_type=jnp.float32)).astype(jnp.bfloat16)
    node_second = jnp.dot(node_hidden, w_node_second, preferred_element_type=jnp.float32)
    node_out = (node_rows.astype(jnp.float32) + layer_norm(node_second, node_gain)).astype(jnp.bfloat16)
    return (node_out.reshape(NLAT, NLON, D), updated.reshape(EDGES, D))
```

```python
import functools

import jax
import jax.numpy as jnp
from jax import lax
from jax.experimental import pallas as pl
from jax.experimental.pallas import tpu as pltpu
from jax.sharding import PartitionSpec as P

F32 = jnp.float32
BF16 = jnp.bfloat16
LANES = 128


def dot(a, b):
    return jnp.dot(a, b, preferred_element_type=F32)


def silu(value):
    half = 0.5 * value
    return half * (1.0 + jnp.tanh(half))


def layer_norm(values, gain_vec):
    average = jnp.mean(values, -1, keepdims=True)
    centred = values - average
    spread = jnp.mean(centred * centred, -1, keepdims=True)
    return centred * lax.rsqrt(spread + 1e-05) * gain_vec


def compute_kernel(
    group,
    block_len,
    tile_nodes,
    tile_ref,
    edge_ref,
    send_ref,
    recv_ref,
    table_ref,
    own_ref,
    w_first_ref,
    w_second_ref,
    edge_gain_ref,
    w_node_first_ref,
    w_node_second_ref,
    node_gain_ref,
    node_out_ref,
    edge_out_ref,
    total_ref,
):
    step = pl.program_id(0)
    features = edge_ref.shape[1]
    table_len = table_ref.shape[0]

    @pl.when(step == 0)
    def _():
        total_ref[...] = jnp.zeros_like(total_ref)

    def columns_of(row, width):
        spread = jnp.broadcast_to(row, (LANES, block_len)).T
        lane = lax.broadcasted_iota(jnp.int32, (block_len, LANES), 1)
        parts = [
            jnp.where(spread == lane + j * LANES, 1.0, 0.0).astype(BF16)
            for j in range(width // LANES)
        ]
        return spread, jnp.concatenate(parts, axis=1)

    sent, received, live = [], [], []
    for i in range(group):
        _, hot = columns_of(send_ref[i], table_len)
        sent.append(hot)
        tile = tile_ref[step * group + i]
        start = pl.multiple_of(tile * tile_nodes, tile_nodes)
        spread, hot_recv = columns_of(recv_ref[i], tile_nodes)
        live.append(jnp.concatenate([spread] * (features // LANES), axis=1))
        received.append(dot(hot_recv, own_ref[pl.ds(start, tile_nodes), :]).astype(BF16))
    edges = edge_ref[...]
    send_rows = dot(jnp.concatenate(sent, axis=0), table_ref[...]).astype(BF16)
    recv_rows = jnp.concatenate(received, axis=0)
    first = (
        dot(edges, w_first_ref[:features, :])
        + dot(recv_rows, w_first_ref[2 * features :, :])
        + dot(send_rows, w_first_ref[features : 2 * features, :])
    )
    hidden = silu(first).astype(BF16)
    message = layer_norm(dot(hidden, w_second_ref[...]), edge_gain_ref[...]).astype(BF16)
    updated = edges.astype(F32) + message.astype(F32)
    edge_out_ref[...] = jnp.where(jnp.concatenate(live, axis=0) >= 0, updated, 0.0).astype(BF16)
    for i in range(group):
        tile = tile_ref[step * group + i]
        start = pl.multiple_of(tile * tile_nodes, tile_nodes)
        node = lax.broadcasted_iota(jnp.int32, (tile_nodes, block_len), 0)
        hot = jnp.where(node == recv_ref[i], 1.0, 0.0).astype(BF16)
        total_ref[pl.ds(start, tile_nodes), :] += dot(
            hot, message[i * block_len : (i + 1) * block_len, :]
        )

    @pl.when(step == pl.num_programs(0) - 1)
    def _():
        own = own_ref[...]
        node_first = dot(own, w_node_first_ref[:features, :]) + dot(
            total_ref[...].astype(BF16), w_node_first_ref[features:, :]
        )
        node_hidden = silu(node_first).astype(BF16)
        node_second = dot(node_hidden, w_node_second_ref[...])
        node_out_ref[...] = (
            own.astype(F32) + layer_norm(node_second, node_gain_ref[...])
        ).astype(BF16)


def compute(
    block_tile, edges, senders, receivers, table, own, weights, tile_nodes
):
    blocks = block_tile.shape[0]
    edge_count, features = edges.shape
    block_len = edge_count // blocks
    node_count = own.shape[0]
    group = 4 if blocks % 4 == 0 else 1
    whole = pl.BlockSpec(memory_space=pltpu.VMEM)
    index = pl.BlockSpec((group, 1, block_len), lambda i, tiles: (i, 0, 0))
    rows = pl.BlockSpec((group * block_len, features), lambda i, tiles: (i, 0))
    return pl.pallas_call(
        functools.partial(compute_kernel, group, block_len, tile_nodes),
        grid_spec=pltpu.PrefetchScalarGridSpec(
            num_scalar_prefetch=1,
            grid=(blocks // group,),
            in_specs=[rows, index, index] + [whole] * 8,
            out_specs=[pl.BlockSpec((node_count, features), lambda i, tiles: (0, 0)), rows],
            scratch_shapes=[pltpu.VMEM((node_count, features), F32)],
        ),
        out_shape=[
            jax.ShapeDtypeStruct((node_count, features), BF16),
            jax.ShapeDtypeStruct((edge_count, features), BF16),
        ],
        compiler_params=pltpu.CompilerParams(
            dimension_semantics=("arbitrary",), vmem_limit_bytes=56 * 1024 * 1024
        ),
    )(
        block_tile,
        edges,
        senders.reshape(blocks, 1, block_len),
        receivers.reshape(blocks, 1, block_len),
        table,
        own,
        *weights,
    )


def shifted(value, axis, step, wrap):
    devices = lax.axis_size(axis)
    pairs = [(i, (i + step) % devices) for i in range(devices) if wrap or 0 <= i + step < devices]
    return lax.ppermute(value, axis, pairs)


def border_rows(own, patch_rows, patch_cols):
    count = patch_rows * patch_cols
    coarse_rows, coarse_cols = patch_rows // 4, patch_cols // 4
    coarse = coarse_rows * coarse_cols
    pick = lax.broadcasted_iota(jnp.int32, (coarse + 2 * patch_rows, count), 0)
    node = lax.broadcasted_iota(jnp.int32, (coarse + 2 * patch_rows, count), 1)
    from_coarse = pick // coarse_cols * 4 * patch_cols + pick % coarse_cols * 4
    side = pick - coarse
    from_side = jnp.where(
        side < patch_rows, side * patch_cols, (side - patch_rows) * patch_cols + patch_cols - 1
    )
    hot = (node == jnp.where(pick < coarse, from_coarse, from_side)).astype(BF16)
    return dot(hot, own).astype(BF16)


def per_device(
    node_latent,
    edge_latent,
    sender,
    receiver,
    block_tile,
    w_first,
    w_second,
    edge_gain,
    w_node_first,
    w_node_second,
    node_gain,
):
    patch_rows, patch_cols, features = node_latent.shape
    lat_count, lon_count = lax.axis_size("lat"), lax.axis_size("lon")
    lat_index, lon_index = lax.axis_index("lat"), lax.axis_index("lon")
    grid_cols = patch_cols * lon_count
    node_count = patch_rows * patch_cols
    coarse_per = patch_rows // 4 * (patch_cols // 4)
    own = node_latent.reshape(node_count, features)
    picked = border_rows(own, patch_rows, patch_cols)
    near, table_len = table_layout(patch_rows, patch_cols, coarse_per * lat_count * lon_count)
    table = build_table(own, picked, patch_rows, patch_cols, near, table_len)

    send_row, send_col = sender // grid_cols, sender % grid_cols
    row = send_row - lat_index * patch_rows
    col = (send_col - lon_index * patch_cols + 1) % grid_cols - 1
    is_near = (row >= -1) & (row <= patch_rows) & (col <= patch_cols)
    inside = (col >= 0) & (col < patch_cols)
    left, right, top, bottom, corners, coarse_at = near
    side = jnp.where(col < 0, left, right)
    corner_side = jnp.where(col < 0, 0, 16)
    top_index = jnp.where(inside, top + col, corners + corner_side + 7)
    bottom_index = jnp.where(inside, bottom + col, corners + corner_side + 8)
    middle = jnp.where(inside, row * patch_cols + col, side + row)
    near_index = jnp.where(row < 0, top_index, jnp.where(row >= patch_rows, bottom_index, middle))
    far_index = (
        coarse_at
        + (send_row // patch_rows * lon_count + send_col // patch_cols) * coarse_per
        + send_row % patch_rows // 4 * (patch_cols // 4)
        + send_col % patch_cols // 4
    )
    senders = jnp.where(sender < 0, -1, jnp.where(is_near, near_index, far_index))
    weights = (
        w_first,
        w_second,
        edge_gain.reshape(1, -1),
        w_node_first,
        w_node_second,
        node_gain.reshape(1, -1),
    )
    node_out, edge_out = compute(
        block_tile, edge_latent, senders, receiver, table, own, weights, 4 * patch_cols
    )
    return node_out.reshape(patch_rows, patch_cols, features), edge_out


def table_layout(patch_rows, patch_cols, coarse_count):
    left = patch_rows * patch_cols
    right = left + patch_rows
    top = right + patch_rows
    bottom = top + patch_cols
    corners = bottom + patch_cols
    coarse_at = corners + 32
    table_len = -(-(coarse_at + coarse_count) // LANES) * LANES
    return (left, right, top, bottom, corners, coarse_at), table_len


def build_table(own, picked, patch_rows, patch_cols, near, table_len):
    features = own.shape[1]
    coarse_per = picked.shape[0] - 2 * patch_rows
    coarse_own = picked[:coarse_per]
    first_col = picked[coarse_per : coarse_per + patch_rows]
    last_col = picked[coarse_per + patch_rows :]
    coarse = lax.all_gather(coarse_own, ("lat", "lon"), axis=0, tiled=True)
    left = shifted(last_col, "lon", 1, True)
    right = shifted(first_col, "lon", -1, True)
    from_north = shifted(
        jnp.concatenate([own[-patch_cols:], left[-8:], right[-8:]]), "lat", 1, False
    )
    from_south = shifted(jnp.concatenate([own[:patch_cols], left[:8], right[:8]]), "lat", -1, False)
    n, nw, ne = from_north[:patch_cols], from_north[patch_cols:-8], from_north[-8:]
    s, sw, se = from_south[:patch_cols], from_south[patch_cols:-8], from_south[-8:]
    pad = jnp.zeros((table_len - near[5] - coarse.shape[0], features), BF16)
    return jnp.concatenate([own, left, right, n, s, nw, sw, ne, se, coarse, pad], axis=0)


def solution(mesh):
    return jax.shard_map(
        per_device,
        mesh=mesh,
        in_specs=(
            P("lat", "lon", None),
            P(("lat", "lon"), None),
            P(("lat", "lon")),
            P(("lat", "lon")),
            P(("lat", "lon")),
            P(),
            P(),
            P(),
            P(),
            P(),
            P(),
        ),
        out_specs=(P("lat", "lon", None), P(("lat", "lon"), None)),
        check_vma=False,
    )
```

```python
import functools

import jax
import jax.numpy as jnp
from jax import lax
from jax.experimental import pallas as pl
from jax.experimental.pallas import tpu as pltpu
from jax.sharding import PartitionSpec as P

F32 = jnp.float32
BF16 = jnp.bfloat16
LANES = 128


def dot(a, b):
    return jnp.dot(a, b, preferred_element_type=F32)


def silu(value):
    half = 0.5 * value
    return half * (1.0 + jnp.tanh(half))


def layer_norm(values, gain_vec):
    average = jnp.mean(values, -1, keepdims=True)
    centred = values - average
    spread = jnp.mean(centred * centred, -1, keepdims=True)
    return centred * lax.rsqrt(spread + 1e-05) * gain_vec


def compute_kernel(
    group,
    block_len,
    tile_nodes,
    tile_ref,
    edge_ref,
    send_ref,
    recv_ref,
    table_ref,
    own_ref,
    w_first_ref,
    w_second_ref,
    edge_gain_ref,
    w_node_first_ref,
    w_node_second_ref,
    node_gain_ref,
    node_out_ref,
    edge_out_ref,
    total_ref,
):
    step = pl.program_id(0)
    features = edge_ref.shape[1]
    node_count = own_ref.shape[0]
    table_len = node_count + table_ref.shape[0]

    @pl.when(step == 0)
    def _():
        total_ref[...] = jnp.zeros_like(total_ref)

    def columns_of(row, width):
        spread = jnp.broadcast_to(row, (LANES, block_len)).T
        lane = lax.broadcasted_iota(jnp.int32, (block_len, LANES), 1)
        parts = [
            jnp.where(spread == lane + j * LANES, 1.0, 0.0).astype(BF16)
            for j in range(width // LANES)
        ]
        return spread, jnp.concatenate(parts, axis=1)

    sent, received, live = [], [], []
    for i in range(group):
        _, hot = columns_of(send_ref[i], table_len)
        sent.append(hot)
        tile = tile_ref[step * group + i]
        start = pl.multiple_of(tile * tile_nodes, tile_nodes)
        spread, hot_recv = columns_of(recv_ref[i], tile_nodes)
        live.append(jnp.concatenate([spread] * (features // LANES), axis=1))
        received.append(dot(hot_recv, own_ref[pl.ds(start, tile_nodes), :]).astype(BF16))
    edges = edge_ref[...]
    sent = jnp.concatenate(sent, axis=0)
    send_rows = (
        dot(sent[:, :node_count], own_ref[...]) + dot(sent[:, node_count:], table_ref[...])
    ).astype(BF16)
    recv_rows = jnp.concatenate(received, axis=0)
    first = (
        dot(edges, w_first_ref[:features, :])
        + dot(recv_rows, w_first_ref[2 * features :, :])
        + dot(send_rows, w_first_ref[features : 2 * features, :])
    )
    hidden = silu(first).astype(BF16)
    message = layer_norm(dot(hidden, w_second_ref[...]), edge_gain_ref[...]).astype(BF16)
    updated = edges.astype(F32) + message.astype(F32)
    edge_out_ref[...] = jnp.where(jnp.concatenate(live, axis=0) >= 0, updated, 0.0).astype(BF16)
    for i in range(group):
        tile = tile_ref[step * group + i]
        start = pl.multiple_of(tile * tile_nodes, tile_nodes)
        node = lax.broadcasted_iota(jnp.int32, (tile_nodes, block_len), 0)
        hot = jnp.where(node == recv_ref[i], 1.0, 0.0).astype(BF16)
        total_ref[pl.ds(start, tile_nodes), :] += dot(
            hot, message[i * block_len : (i + 1) * block_len, :]
        )

    @pl.when(step == pl.num_programs(0) - 1)
    def _():
        own = own_ref[...]
        node_first = dot(own, w_node_first_ref[:features, :]) + dot(
            total_ref[...].astype(BF16), w_node_first_ref[features:, :]
        )
        node_hidden = silu(node_first).astype(BF16)
        node_second = dot(node_hidden, w_node_second_ref[...])
        node_out_ref[...] = (
            own.astype(F32) + layer_norm(node_second, node_gain_ref[...])
        ).astype(BF16)


def compute(
    block_tile, edges, senders, receivers, table, own, weights, tile_nodes
):
    blocks = block_tile.shape[0]
    edge_count, features = edges.shape
    block_len = edge_count // blocks
    node_count = own.shape[0]
    group = 4 if blocks % 4 == 0 else 1
    whole = pl.BlockSpec(memory_space=pltpu.VMEM)
    index = pl.BlockSpec((group, 1, block_len), lambda i, tiles: (i, 0, 0))
    rows = pl.BlockSpec((group * block_len, features), lambda i, tiles: (i, 0))
    return pl.pallas_call(
        functools.partial(compute_kernel, group, block_len, tile_nodes),
        grid_spec=pltpu.PrefetchScalarGridSpec(
            num_scalar_prefetch=1,
            grid=(blocks // group,),
            in_specs=[rows, index, index] + [whole] * 8,
            out_specs=[pl.BlockSpec((node_count, features), lambda i, tiles: (0, 0)), rows],
            scratch_shapes=[pltpu.VMEM((node_count, features), F32)],
        ),
        out_shape=[
            jax.ShapeDtypeStruct((node_count, features), BF16),
            jax.ShapeDtypeStruct((edge_count, features), BF16),
        ],
        compiler_params=pltpu.CompilerParams(
            dimension_semantics=("arbitrary",), vmem_limit_bytes=56 * 1024 * 1024
        ),
    )(
        block_tile,
        edges,
        senders.reshape(blocks, 1, block_len),
        receivers.reshape(blocks, 1, block_len),
        table,
        own,
        *weights,
    )


def border_rows(own, patch_rows, patch_cols):
    count = patch_rows * patch_cols
    coarse_rows, coarse_cols = patch_rows // 4, patch_cols // 4
    coarse = coarse_rows * coarse_cols
    pick = lax.broadcasted_iota(jnp.int32, (coarse + 2 * patch_rows, count), 0)
    node = lax.broadcasted_iota(jnp.int32, (coarse + 2 * patch_rows, count), 1)
    from_coarse = pick // coarse_cols * 4 * patch_cols + pick % coarse_cols * 4
    side = pick - coarse
    from_side = jnp.where(
        side < patch_rows, side * patch_cols, (side - patch_rows) * patch_cols + patch_cols - 1
    )
    hot = (node == jnp.where(pick < coarse, from_coarse, from_side)).astype(BF16)
    return dot(hot, own).astype(BF16)


def per_device(
    node_latent,
    edge_latent,
    sender,
    receiver,
    block_tile,
    w_first,
    w_second,
    edge_gain,
    w_node_first,
    w_node_second,
    node_gain,
):
    patch_rows, patch_cols, features = node_latent.shape
    lat_count, lon_count = lax.axis_size("lat"), lax.axis_size("lon")
    lat_index, lon_index = lax.axis_index("lat"), lax.axis_index("lon")
    grid_cols = patch_cols * lon_count
    node_count = patch_rows * patch_cols
    coarse_per = patch_rows // 4 * (patch_cols // 4)
    own = node_latent.reshape(node_count, features)
    picked = border_rows(own, patch_rows, patch_cols)
    near, table_len = table_layout(patch_rows, patch_cols, coarse_per * lat_count * lon_count)
    table = build_table(own, picked, patch_rows, patch_cols, near, table_len)

    send_row, send_col = sender // grid_cols, sender % grid_cols
    row = send_row - lat_index * patch_rows
    col = (send_col - lon_index * patch_cols + 1) % grid_cols - 1
    is_near = (row >= -1) & (row <= patch_rows) & (col <= patch_cols)
    inside = (col >= 0) & (col < patch_cols)
    left, right, top, bottom, corners, coarse_at = near
    side = jnp.where(col < 0, left, right)
    corner_side = jnp.where(col < 0, 0, 16)
    top_index = jnp.where(inside, top + col, corners + corner_side + 7)
    bottom_index = jnp.where(inside, bottom + col, corners + corner_side + 8)
    middle = jnp.where(inside, row * patch_cols + col, side + row)
    near_index = jnp.where(row < 0, top_index, jnp.where(row >= patch_rows, bottom_index, middle))
    far_index = (
        coarse_at
        + (send_row // patch_rows * lon_count + send_col // patch_cols) * coarse_per
        + send_row % patch_rows // 4 * (patch_cols // 4)
        + send_col % patch_cols // 4
    )
    senders = jnp.where(sender < 0, -1, jnp.where(is_near, near_index, far_index))
    weights = (
        w_first,
        w_second,
        edge_gain.reshape(1, -1),
        w_node_first,
        w_node_second,
        node_gain.reshape(1, -1),
    )
    node_out, edge_out = compute(
        block_tile, edge_latent, senders, receiver, table, own, weights, 4 * patch_cols
    )
    return node_out.reshape(patch_rows, patch_cols, features), edge_out


def table_layout(patch_rows, patch_cols, coarse_count):
    left = patch_rows * patch_cols
    right = left + patch_rows
    top = right + patch_rows
    bottom = top + patch_cols
    corners = bottom + patch_cols
    coarse_at = corners + 32
    table_len = -(-(coarse_at + coarse_count) // LANES) * LANES
    return (left, right, top, bottom, corners, coarse_at), table_len


def exchange_kernel(patch_rows, patch_cols, near, own_ref, picked_ref, table_ref, *sems):
    halo_send, halo_recv, far_send, far_recv, pair_send, pair_recv, ready = sems
    lat_count, lon_count = lax.axis_size("lat"), lax.axis_size("lon")
    lat, lon = lax.axis_index("lat"), lax.axis_index("lon")
    node_count = own_ref.shape[0]
    left, right, top, bottom, corners, coarse_at = near
    per = picked_ref.shape[0] - 2 * patch_rows
    cores = 2 if lat_count % 2 == 0 else 1
    chips = lat_count * lon_count // cores
    core = lax.rem(lat, cores)
    chip = lax.div(lat, cores) * lon_count + lon

    def place(which, on_core):
        return lax.div(which, lon_count) * cores + on_core, lax.rem(which, lon_count)

    def slot(which, on_core):
        at_lat, at_lon = place(which, on_core)
        start = coarse_at + (at_lat * lon_count + at_lon) * per
        return table_ref.at[pl.ds(pl.multiple_of(start, 8), per), :]

    def copy(source, target, send_sem, recv_sem, at_lat, at_lon):
        return pltpu.make_async_remote_copy(
            src_ref=source,
            dst_ref=target,
            send_sem=send_sem,
            recv_sem=recv_sem,
            device_id={"lat": at_lat, "lon": at_lon},
            device_id_type=pl.DeviceIdType.MESH,
        )

    coarse_own = picked_ref.at[pl.ds(0, per), :]

    def far_out(k):
        at_lat, at_lon = place(lax.rem(chip + k, chips), core)
        return copy(coarse_own, slot(chip, core), far_send.at[k], far_recv.at[k], at_lat, at_lon)

    def far_in(k):
        origin = lax.rem(chip + chips - k, chips)
        at_lat, at_lon = place(origin, core)
        return copy(coarse_own, slot(origin, core), far_send.at[k], far_recv.at[k], at_lat, at_lon)

    def pair(k, source_core):
        origin = lax.rem(chip + chips - k, chips)
        block = slot(origin, source_core)
        return copy(block, block, pair_send.at[k], pair_recv.at[k], lat + 1 - 2 * core, lon)

    first, last = per, per + patch_rows
    halos = (
        (picked_ref, last, patch_rows, left, 0, 1),
        (picked_ref, first, patch_rows, right, 0, -1),
        (own_ref, node_count - patch_cols, patch_cols, top, 1, 0),
        (own_ref, 0, patch_cols, bottom, -1, 0),
        (picked_ref, last + patch_rows - 8, 8, corners, 1, 1),
        (picked_ref, last, 8, corners + 8, -1, 1),
        (picked_ref, first + patch_rows - 8, 8, corners + 16, 1, -1),
        (picked_ref, first, 8, corners + 24, -1, -1),
    )

    def halo(i):
        ref, start, size, target, step_lat, step_lon = halos[i]
        at_lat = lax.rem(lat + step_lat + lat_count, lat_count)
        at_lon = lax.rem(lon + step_lon + lon_count, lon_count)
        return copy(
            ref.at[start : start + size, :],
            table_ref.at[target : target + size, :],
            halo_send.at[i],
            halo_recv.at[i],
            at_lat,
            at_lon,
        )

    def sends(i):
        there = lat + halos[i][4]
        return (there >= 0) & (there < lat_count)

    def receives(i):
        origin = lat - halos[i][4]
        return (origin >= 0) & (origin < lat_count)

    lax.fori_loop(1, chips, lambda k, c: (far_out(k).start(), c)[1], 0)
    if cores == 2:
        own_pair = copy(
            coarse_own, slot(chip, core), pair_send.at[0], pair_recv.at[0], lat + 1 - 2 * core, lon
        )
        own_pair.start()
    for i in range(len(halos)):
        pl.when(sends(i))(lambda i=i: halo(i).start())

    local = pltpu.make_async_copy(coarse_own, slot(chip, core), ready)
    local.start()
    for i, (_, _, size, target, _, _) in enumerate(halos):

        @pl.when(jnp.logical_not(receives(i)))
        def _():
            table_ref[target : target + size, :] = jnp.zeros((size, table_ref.shape[1]), BF16)

    used = coarse_at + lat_count * lon_count * per
    if used < table_ref.shape[0]:
        table_ref[used:, :] = jnp.zeros((table_ref.shape[0] - used, table_ref.shape[1]), BF16)

    def relay(k, c):
        far_in(k).wait_recv()
        if cores == 2:
            pair(k, core).start()
        return c

    lax.fori_loop(1, chips, relay, 0)
    local.wait()
    for i in range(len(halos)):
        pl.when(receives(i))(lambda i=i: halo(i).wait_recv())
        pl.when(sends(i))(lambda i=i: halo(i).wait_send())

    def finish(k, c):
        far_out(k).wait_send()
        if cores == 2:
            pair(k, core).wait_send()
            pair(k, 1 - core).wait_recv()
        return c

    lax.fori_loop(1, chips, finish, 0)
    if cores == 2:
        own_pair.wait_send()
        pair(0, 1 - core).wait_recv()


def build_table(own, picked, patch_rows, patch_cols, near, table_len):
    offset = own.shape[0]
    near = tuple(at - offset for at in near)
    chips = lax.axis_size("lat") * lax.axis_size("lon")
    sems = [pltpu.SemaphoreType.DMA((8,))] * 2 + [pltpu.SemaphoreType.DMA((chips,))] * 4
    return pl.pallas_call(
        functools.partial(exchange_kernel, patch_rows, patch_cols, near),
        in_specs=[pl.BlockSpec(memory_space=pltpu.VMEM)] * 2,
        out_specs=pl.BlockSpec(memory_space=pltpu.VMEM),
        out_shape=jax.ShapeDtypeStruct((table_len - offset, own.shape[1]), BF16),
        scratch_shapes=sems + [pltpu.SemaphoreType.DMA],
        compiler_params=pltpu.CompilerParams(
            has_side_effects=True, vmem_limit_bytes=24 * 1024 * 1024
        ),
    )(own, picked)


def solution(mesh):
    return jax.shard_map(
        per_device,
        mesh=mesh,
        in_specs=(
            P("lat", "lon", None),
            P(("lat", "lon"), None),
            P(("lat", "lon")),
            P(("lat", "lon")),
            P(("lat", "lon")),
            P(),
            P(),
            P(),
            P(),
            P(),
            P(),
        ),
        out_specs=(P("lat", "lon", None), P(("lat", "lon"), None)),
        check_vma=False,
    )
```

```python
import functools

import jax
import jax.numpy as jnp
from jax import lax
from jax.experimental import pallas as pl
from jax.experimental.pallas import tpu as pltpu
from jax.sharding import PartitionSpec as P

F32 = jnp.float32
BF16 = jnp.bfloat16
LANES = 128


def dot(a, b):
    return jnp.dot(a, b, preferred_element_type=F32)


def silu(value):
    half = 0.5 * value
    return half * (1.0 + jnp.tanh(half))


def layer_norm(values, gain_vec):
    average = jnp.mean(values, -1, keepdims=True)
    centred = values - average
    spread = jnp.mean(centred * centred, -1, keepdims=True)
    return centred * lax.rsqrt(spread + 1e-05) * gain_vec


def compute_kernel(
    group,
    block_len,
    tile_nodes,
    tile_ref,
    edge_ref,
    send_ref,
    recv_ref,
    table_ref,
    own_ref,
    w_first_ref,
    w_second_ref,
    edge_gain_ref,
    w_node_first_ref,
    w_node_second_ref,
    node_gain_ref,
    node_out_ref,
    edge_out_ref,
    total_ref,
):
    step = pl.program_id(0)
    features = edge_ref.shape[1]
    node_count = own_ref.shape[0]
    table_len = node_count + table_ref.shape[0]

    @pl.when(step == 0)
    def _():
        total_ref[...] = jnp.zeros_like(total_ref)

    def columns_of(row, width):
        spread = jnp.broadcast_to(row, (LANES, block_len)).T
        lane = lax.broadcasted_iota(jnp.int32, (block_len, LANES), 1)
        parts = [
            jnp.where(spread == lane + j * LANES, 1.0, 0.0).astype(BF16)
            for j in range(width // LANES)
        ]
        return spread, jnp.concatenate(parts, axis=1)

    sent, received, live = [], [], []
    for i in range(group):
        _, hot = columns_of(send_ref[i], table_len)
        sent.append(hot)
        tile = tile_ref[step * group + i]
        start = pl.multiple_of(tile * tile_nodes, tile_nodes)
        spread, hot_recv = columns_of(recv_ref[i], tile_nodes)
        live.append(jnp.concatenate([spread] * (features // LANES), axis=1))
        received.append(dot(hot_recv, own_ref[pl.ds(start, tile_nodes), :]).astype(BF16))
    edges = edge_ref[...]
    sent = jnp.concatenate(sent, axis=0)
    send_rows = (
        dot(sent[:, :node_count], own_ref[...]) + dot(sent[:, node_count:], table_ref[...])
    ).astype(BF16)
    recv_rows = jnp.concatenate(received, axis=0)
    first = (
        dot(edges, w_first_ref[:features, :])
        + dot(recv_rows, w_first_ref[2 * features :, :])
        + dot(send_rows, w_first_ref[features : 2 * features, :])
    )
    hidden = silu(first).astype(BF16)
    message = layer_norm(dot(hidden, w_second_ref[...]), edge_gain_ref[...]).astype(BF16)
    updated = edges.astype(F32) + message.astype(F32)
    edge_out_ref[...] = jnp.where(jnp.concatenate(live, axis=0) >= 0, updated, 0.0).astype(BF16)
    for i in range(group):
        tile = tile_ref[step * group + i]
        start = pl.multiple_of(tile * tile_nodes, tile_nodes)
        node = lax.broadcasted_iota(jnp.int32, (tile_nodes, block_len), 0)
        hot = jnp.where(node == recv_ref[i], 1.0, 0.0).astype(BF16)
        total_ref[pl.ds(start, tile_nodes), :] += dot(
            hot, message[i * block_len : (i + 1) * block_len, :]
        )

    @pl.when(step == pl.num_programs(0) - 1)
    def _():
        own = own_ref[...]
        node_first = dot(own, w_node_first_ref[:features, :]) + dot(
            total_ref[...].astype(BF16), w_node_first_ref[features:, :]
        )
        node_hidden = silu(node_first).astype(BF16)
        node_second = dot(node_hidden, w_node_second_ref[...])
        node_out_ref[...] = (
            own.astype(F32) + layer_norm(node_second, node_gain_ref[...])
        ).astype(BF16)


def compute(
    block_tile, edges, senders, receivers, table, own, weights, tile_nodes
):
    blocks = block_tile.shape[0]
    edge_count, features = edges.shape
    block_len = edge_count // blocks
    node_count = own.shape[0]
    group = 4 if blocks % 4 == 0 else 1
    whole = pl.BlockSpec(memory_space=pltpu.VMEM)
    index = pl.BlockSpec((group, 1, block_len), lambda i, tiles: (i, 0, 0))
    rows = pl.BlockSpec((group * block_len, features), lambda i, tiles: (i, 0))
    return pl.pallas_call(
        functools.partial(compute_kernel, group, block_len, tile_nodes),
        grid_spec=pltpu.PrefetchScalarGridSpec(
            num_scalar_prefetch=1,
            grid=(blocks // group,),
            in_specs=[rows, index, index] + [whole] * 8,
            out_specs=[pl.BlockSpec((node_count, features), lambda i, tiles: (0, 0)), rows],
            scratch_shapes=[pltpu.VMEM((node_count, features), F32)],
        ),
        out_shape=[
            jax.ShapeDtypeStruct((node_count, features), BF16),
            jax.ShapeDtypeStruct((edge_count, features), BF16),
        ],
        compiler_params=pltpu.CompilerParams(
            dimension_semantics=("arbitrary",), vmem_limit_bytes=50 * 1024 * 1024
        ),
    )(
        block_tile,
        edges,
        senders.reshape(blocks, 1, block_len),
        receivers.reshape(blocks, 1, block_len),
        table,
        own,
        *weights,
    )


def border_rows(own, patch_rows, patch_cols):
    count = patch_rows * patch_cols
    coarse_rows, coarse_cols = patch_rows // 4, patch_cols // 4
    coarse = coarse_rows * coarse_cols
    pick = lax.broadcasted_iota(jnp.int32, (coarse + 2 * patch_rows, count), 0)
    node = lax.broadcasted_iota(jnp.int32, (coarse + 2 * patch_rows, count), 1)
    from_coarse = pick // coarse_cols * 4 * patch_cols + pick % coarse_cols * 4
    side = pick - coarse
    from_side = jnp.where(
        side < patch_rows, side * patch_cols, (side - patch_rows) * patch_cols + patch_cols - 1
    )
    hot = (node == jnp.where(pick < coarse, from_coarse, from_side)).astype(BF16)
    return dot(hot, own).astype(BF16)


def per_device(
    node_latent,
    edge_latent,
    sender,
    receiver,
    block_tile,
    w_first,
    w_second,
    edge_gain,
    w_node_first,
    w_node_second,
    node_gain,
):
    patch_rows, patch_cols, features = node_latent.shape
    lat_count, lon_count = lax.axis_size("lat"), lax.axis_size("lon")
    lat_index, lon_index = lax.axis_index("lat"), lax.axis_index("lon")
    grid_cols = patch_cols * lon_count
    node_count = patch_rows * patch_cols
    coarse_per = patch_rows // 4 * (patch_cols // 4)
    own = node_latent.reshape(node_count, features)
    picked = border_rows(own, patch_rows, patch_cols)
    near, table_len = table_layout(patch_rows, patch_cols, coarse_per * lat_count * lon_count)
    table = build_table(own, picked, patch_rows, patch_cols, near, table_len)

    send_row, send_col = sender // grid_cols, sender % grid_cols
    row = send_row - lat_index * patch_rows
    col = (send_col - lon_index * patch_cols + 1) % grid_cols - 1
    is_near = (row >= -1) & (row <= patch_rows) & (col <= patch_cols)
    inside = (col >= 0) & (col < patch_cols)
    left, right, top, bottom, corners, coarse_at = near
    side = jnp.where(col < 0, left, right)
    corner_side = jnp.where(col < 0, 0, 16)
    top_index = jnp.where(inside, top + col, corners + corner_side + 7)
    bottom_index = jnp.where(inside, bottom + col, corners + corner_side + 8)
    middle = jnp.where(inside, row * patch_cols + col, side + row)
    near_index = jnp.where(row < 0, top_index, jnp.where(row >= patch_rows, bottom_index, middle))
    far_index = (
        coarse_at
        + (send_row // patch_rows * lon_count + send_col // patch_cols) * coarse_per
        + send_row % patch_rows // 4 * (patch_cols // 4)
        + send_col % patch_cols // 4
    )
    senders = jnp.where(sender < 0, -1, jnp.where(is_near, near_index, far_index))
    weights = (
        w_first,
        w_second,
        edge_gain.reshape(1, -1),
        w_node_first,
        w_node_second,
        node_gain.reshape(1, -1),
    )
    node_out, edge_out = compute(
        block_tile, edge_latent, senders, receiver, table, own, weights, 4 * patch_cols
    )
    return node_out.reshape(patch_rows, patch_cols, features), edge_out


def table_layout(patch_rows, patch_cols, coarse_count):
    left = patch_rows * patch_cols
    right = left + patch_rows
    top = right + patch_rows
    bottom = top + patch_cols
    corners = bottom + patch_cols
    coarse_at = corners + 32
    table_len = -(-(coarse_at + coarse_count) // LANES) * LANES
    return (left, right, top, bottom, corners, coarse_at), table_len


def exchange_kernel(patch_rows, patch_cols, near, own_ref, picked_ref, table_ref, *sems):
    halo_send, halo_recv, far_send, far_recv, pair_send, pair_recv, ready = sems
    lat_count, lon_count = lax.axis_size("lat"), lax.axis_size("lon")
    lat, lon = lax.axis_index("lat"), lax.axis_index("lon")
    node_count = own_ref.shape[0]
    left, right, top, bottom, corners, coarse_at = near
    per = picked_ref.shape[0] - 2 * patch_rows
    cores = 2 if lat_count % 2 == 0 else 1
    chips = lat_count * lon_count // cores
    core = lax.rem(lat, cores)
    chip = lax.div(lat, cores) * lon_count + lon

    def place(which, on_core):
        return lax.div(which, lon_count) * cores + on_core, lax.rem(which, lon_count)

    def slot(which, on_core):
        at_lat, at_lon = place(which, on_core)
        start = coarse_at + (at_lat * lon_count + at_lon) * per
        return table_ref.at[pl.ds(pl.multiple_of(start, 8), per), :]

    def copy(source, target, send_sem, recv_sem, at_lat, at_lon):
        return pltpu.make_async_remote_copy(
            src_ref=source,
            dst_ref=target,
            send_sem=send_sem,
            recv_sem=recv_sem,
            device_id={"lat": at_lat, "lon": at_lon},
            device_id_type=pl.DeviceIdType.MESH,
        )

    coarse_own = picked_ref.at[pl.ds(0, per), :]

    def far_out(k):
        at_lat, at_lon = place(lax.rem(chip + k, chips), core)
        return copy(coarse_own, slot(chip, core), far_send.at[k], far_recv.at[k], at_lat, at_lon)

    def far_in(k):
        origin = lax.rem(chip + chips - k, chips)
        at_lat, at_lon = place(origin, core)
        return copy(coarse_own, slot(origin, core), far_send.at[k], far_recv.at[k], at_lat, at_lon)

    def pair(k, source_core):
        origin = lax.rem(chip + chips - k, chips)
        block = slot(origin, source_core)
        return copy(block, block, pair_send.at[k], pair_recv.at[k], lat + 1 - 2 * core, lon)

    first, last = per, per + patch_rows
    halos = (
        (picked_ref, last, patch_rows, left, 0, 1),
        (picked_ref, first, patch_rows, right, 0, -1),
        (own_ref, node_count - patch_cols, patch_cols, top, 1, 0),
        (own_ref, 0, patch_cols, bottom, -1, 0),
        (picked_ref, last + patch_rows - 8, 8, corners, 1, 1),
        (picked_ref, last, 8, corners + 8, -1, 1),
        (picked_ref, first + patch_rows - 8, 8, corners + 16, 1, -1),
        (picked_ref, first, 8, corners + 24, -1, -1),
    )

    def halo(i):
        ref, start, size, target, step_lat, step_lon = halos[i]
        at_lat = lax.rem(lat + step_lat + lat_count, lat_count)
        at_lon = lax.rem(lon + step_lon + lon_count, lon_count)
        return copy(
            ref.at[start : start + size, :],
            table_ref.at[target : target + size, :],
            halo_send.at[i],
            halo_recv.at[i],
            at_lat,
            at_lon,
        )

    def sends(i):
        there = lat + halos[i][4]
        return (there >= 0) & (there < lat_count)

    def receives(i):
        origin = lat - halos[i][4]
        return (origin >= 0) & (origin < lat_count)

    lax.fori_loop(1, chips, lambda k, c: (far_out(k).start(), c)[1], 0)
    if cores == 2:
        own_pair = copy(
            coarse_own, slot(chip, core), pair_send.at[0], pair_recv.at[0], lat + 1 - 2 * core, lon
        )
        own_pair.start()
    for i in range(len(halos)):
        pl.when(sends(i))(lambda i=i: halo(i).start())

    local = pltpu.make_async_copy(coarse_own, slot(chip, core), ready)
    local.start()
    for i, (_, _, size, target, _, _) in enumerate(halos):

        @pl.when(jnp.logical_not(receives(i)))
        def _():
            table_ref[target : target + size, :] = jnp.zeros((size, table_ref.shape[1]), BF16)

    used = coarse_at + lat_count * lon_count * per
    if used < table_ref.shape[0]:
        table_ref[used:, :] = jnp.zeros((table_ref.shape[0] - used, table_ref.shape[1]), BF16)

    def relay(k, c):
        far_in(k).wait_recv()
        if cores == 2:
            pair(k, core).start()
        return c

    lax.fori_loop(1, chips, relay, 0)
    local.wait()
    for i in range(len(halos)):
        pl.when(receives(i))(lambda i=i: halo(i).wait_recv())
        pl.when(sends(i))(lambda i=i: halo(i).wait_send())

    def finish(k, c):
        far_out(k).wait_send()
        if cores == 2:
            pair(k, core).wait_send()
            pair(k, 1 - core).wait_recv()
        return c

    lax.fori_loop(1, chips, finish, 0)
    if cores == 2:
        own_pair.wait_send()
        pair(0, 1 - core).wait_recv()


def build_table(own, picked, patch_rows, patch_cols, near, table_len):
    offset = own.shape[0]
    near = tuple(at - offset for at in near)
    chips = lax.axis_size("lat") * lax.axis_size("lon")
    sems = [pltpu.SemaphoreType.DMA((8,))] * 2 + [pltpu.SemaphoreType.DMA((chips,))] * 4
    return pl.pallas_call(
        functools.partial(exchange_kernel, patch_rows, patch_cols, near),
        in_specs=[pl.BlockSpec(memory_space=pltpu.VMEM)] * 2,
        out_specs=pl.BlockSpec(memory_space=pltpu.VMEM),
        out_shape=jax.ShapeDtypeStruct((table_len - offset, own.shape[1]), BF16),
        scratch_shapes=sems + [pltpu.SemaphoreType.DMA],
        compiler_params=pltpu.CompilerParams(
            has_side_effects=True, vmem_limit_bytes=16 * 1024 * 1024
        ),
        cost_estimate=pl.CostEstimate(
            flops=0, bytes_accessed=40 * chips * own.size // 16, transcendentals=0
        ),
    )(own, picked)


def solution(mesh):
    return jax.shard_map(
        per_device,
        mesh=mesh,
        in_specs=(
            P("lat", "lon", None),
            P(("lat", "lon"), None),
            P(("lat", "lon")),
            P(("lat", "lon")),
            P(("lat", "lon")),
            P(),
            P(),
            P(),
            P(),
            P(),
            P(),
        ),
        out_specs=(P("lat", "lon", None), P(("lat", "lon"), None)),
        check_vma=False,
    )
```
